32 devices in a mesh: groups: 2 (over x), mp: 8 (over z, y), row: 2 (over core).
Axes of the slice: x: 2, y: 2, z: 4, core: 2. Of those that a mesh axis runs over, the one named last changes fastest.
Arguments:
- stream: bfloat16 [2, 256, 4096], P(None, ('groups', 'row'), 'mp'), parts along dimension 1, may hold values from -12 to 12
- projected: bfloat16 [2, 256, 2, 8192], P(None, ('groups', 'row'), None, 'mp'), parts along dimension 1, may hold values from -6 to 6
- conv_state: bfloat16 [256, 3, 8192], P(('groups', 'row'), None, 'mp'), parts along dimension 0, may hold values from -6 to 6
- scan_state: float32 [256, 16, 8192], P(('groups', 'row'), None, 'mp'), parts along dimension 0, may hold values from -6 to 6
- conv_weight: float32 [4, 8192], P(None, 'mp'), may hold values from -3 to 3
- conv_bias: float32 [8192], P('mp'), may hold values from -3 to 3
- state_proj: bfloat16 [8192, 288], P('mp'), may hold values from -0.0625 to 0.0625
- step_proj: bfloat16 [256, 8192], P(None, 'mp'), may hold values from -0.375 to 0.375
- step_bias: float32 [8192], P('mp'), may hold values from -3 to 0.5
- decay_log: float32 [16, 8192], P(None, 'mp'), may hold values from -4 to 2
- skip_gain: float32 [8192], P('mp'), may hold values from 0.25 to 1.75
- out_weight: bfloat16 [8192, 4096], P('mp'), may hold values from -0.09375 to 0.09375
- norm_gain: float32 [4096], replicated, may hold values from 0.25 to 1.75
- router: bfloat16 [16, 4096], replicated, may hold values from -0.09375 to 0.09375
- expert_gate: bfloat16 [2, 4096, 12288], P('row', None, 'mp'), may hold values from -0.09375 to 0.09375
- expert_up: bfloat16 [2, 4096, 12288], P('row', None, 'mp'), may hold values from -0.09375 to 0.09375
- expert_down: bfloat16 [2, 12288, 4096], P('row', 'mp'), may hold values from -0.078125 to 0.078125
- expert_ids: int32 [2, 256, 2], P(None, ('groups', 'row')), parts along dimension 1, may hold values from 0 to 15, as said below
Outputs:
- mixed_out: bfloat16 [2, 256, 4096], P(None, ('groups', 'row'), 'mp'), parts along dimension 1
- new_state: float32 [256, 16, 8192], P(('groups', 'row'), None, 'mp'), parts along dimension 0
The draws below stay inside these ranges and needn't reach their ends.
There are 2 independent parts, one for each index of `groups`. The reference program is written for one: setup_inputs(seed, part) draws one part's arguments, and reference() takes and returns one part's arrays. A program takes and returns all parts, laid end to end along the dimension named above; an argument that names none is the same for every part. Nothing has to cross between parts.
Inputs may be any that keep to these rules, and one draw needn't show every extreme that they name: `expert_ids`: A row's two ids differ. In each step, at most 16 of the rows of one device (aligned blocks of 64 rows) choose expert 0, and at most 16 choose expert 1; in every draw some step has exactly 16 such rows for both experts in every block.
All inputs are finite; a program needn't handle non-finite values.
Results may differ from the reference program's by a relative error of at most 0.006.
Values may be sent and summed in bfloat16 or wider, within the bound.
A program may use at most 128 MiB of HBM per device.

```python
import math
import jax
import jax.numpy as jnp
from jax import lax

D = 4096
DI = 8192
DTR = 256
NS = 16
KC = 4
EXPERTS = 16
TOPK = 2
FF = 12288
STEPS = 2
ROWS_DEV = 64
CAP = 16
ROWS = 128
FLIGHT = 2


def draw_stream(key, part):
    base_key = jax.random.fold_in(key, 101)
    key_list = jax.random.split(base_key, 3)
    row_scale = jnp.exp(jax.random.uniform(key_list[1], (STEPS, ROWS, 1), jnp.float32, math.log(0.3), math.log(3.0)))
    col_scale = jnp.exp(jax.random.uniform(key_list[2], (1, 1, D), jnp.float32, math.log(0.3), math.log(3.0)))
    noise_part = jax.random.normal(key_list[0], (STEPS, ROWS, D), jnp.float32)
    return jnp.clip(noise_part * row_scale * col_scale, -12.0, 12.0).astype(jnp.bfloat16)


def draw_expert_ids(key, part):
    base_key = jax.random.fold_in(key, 202)
    key_list = jax.random.split(base_key, 8)
    block_count = ROWS // ROWS_DEV
    first_count = jax.random.randint(key_list[0], (STEPS, block_count), 1, CAP + 1)
    second_count = jax.random.randint(key_list[1], (STEPS, block_count), 1, CAP + 1)
    full_step = jax.random.randint(key_list[2], (), 0, STEPS)
    is_full = jnp.arange(STEPS)[:, None] == full_step
    first_count = jnp.where(is_full, CAP, first_count)
    second_count = jnp.where(is_full, CAP, second_count)
    first_keys = jax.random.split(key_list[3], STEPS * block_count)
    second_keys = jax.random.split(key_list[4], STEPS * block_count)
    first_rank = jax.vmap(lambda one_key: jax.random.permutation(one_key, ROWS_DEV))(first_keys).reshape(STEPS, block_count, ROWS_DEV)
    second_rank = jax.vmap(lambda one_key: jax.random.permutation(one_key, ROWS_DEV))(second_keys).reshape(STEPS, block_count, ROWS_DEV)
    in_first = first_rank < first_count[:, :, None]
    in_second = second_rank < second_count[:, :, None]
    other_one = 2 + jax.random.randint(key_list[5], (STEPS, block_count, ROWS_DEV), 0, EXPERTS - 2)
    other_two = 2 + (other_one - 2 + 1 + jax.random.randint(key_list[6], (STEPS, block_count, ROWS_DEV), 0, EXPERTS - 3)) % (EXPERTS - 2)
    column_one = jnp.where(in_first, 0, other_one)
    column_two = jnp.where(in_second, 1, other_two)
    swapped = jax.random.randint(key_list[7], (STEPS, block_count, ROWS_DEV), 0, 2) == 1
    left_side = jnp.where(swapped, column_two, column_one)
    right_side = jnp.where(swapped, column_one, column_two)
    return jnp.stack([left_side, right_side], axis=-1).reshape(STEPS, ROWS, 2).astype(jnp.int32)


def with_spikes(entries, stream_key, source, target, parts, factor):
    owner, partner = [(jnp.arange(entries.shape[dim]) // (entries.shape[dim] // parts)).reshape([-1 if axis == dim else 1 for axis in range(entries.ndim)]) for dim in (source, target)]
    chosen = jax.random.permutation(stream_key, parts)[partner]
    strong = (owner == chosen) | (owner == (partner + parts // 2) % parts)
    return jnp.where(strong, factor * entries, entries)


def block_levels(key, dims, shards, least, largest):
    gain, own = 1.0, jax.random.fold_in(key, 6)
    for position, parts in shards:
        draws = jnp.exp(jax.random.uniform(jax.random.fold_in(own, position), (parts,), jnp.float32, least / len(shards), largest / len(shards)))
        gain = gain * jnp.repeat(draws, dims[position] // parts).reshape([-1 if axis == position else 1 for axis in range(len(dims))])
    return gain


def noise(rng, shape, deviation, most, cuts=(), held_as=jnp.bfloat16):
    drawn = jax.random.normal(rng, shape, jnp.float32) * deviation
    if len(cuts) > 0:
        drawn = block_levels(rng, shape, cuts, -0.22, 0.18) * drawn
    return jnp.clip(drawn, min=-most, max=most).astype(held_as)


def gaussian_with(own_key, dims, scale, bound, shards, heavy, kind=jnp.bfloat16):
    array = scale * jax.random.normal(own_key, dims, jnp.float32)
    if shards:
        array = array * block_levels(own_key, dims, shards, -0.22, 0.18)
    return jnp.clip(with_spikes(array, jax.random.fold_in(own_key, 3), *heavy), -bound, bound).astype(kind)


def setup_inputs(seed: int = 0, part: int = 0) -> dict:
    seeds = jax.random.split(jax.random.key(seed), 19)
    part_keys = jax.random.split(jax.random.fold_in(seeds[18], part), 19)
    stream = draw_stream(jax.random.fold_in(jax.random.fold_in(seeds[18], part), 71), part)
    projected = noise(part_keys[1], (STEPS, ROWS, 2, DI), 1.0, 6.0, ((1, 2), (3, 8)))
    conv_state = noise(part_keys[2], (ROWS, KC - 1, DI), 1.0, 6.0, ((0, 2), (2, 8)))
    scan_state = noise(part_keys[3], (ROWS, NS, DI), 1.0, 6.0, ((0, 2), (2, 8)), jnp.float32)
    conv_weight = noise(seeds[4], (KC, DI), KC ** -0.5, 3.0, ((1, 8),), jnp.float32)
    conv_bias = noise(seeds[5], (DI,), 0.5, 3.0, ((0, 8),), jnp.float32)
    state_proj = noise(seeds[6], (DI, DTR + 2 * NS), DI ** -0.5, 0.0625, ((0, 8),))
    step_proj = noise(seeds[7], (DTR, DI), DTR ** -0.5, 0.375, ((1, 8),))
    step_bias = jnp.clip(-3.0 + 3.5 * jax.random.uniform(seeds[8], (DI,), jnp.float32) ** block_levels(seeds[8], (DI,), ((0, 8),), -0.2, 0.2), -3.0, 0.5)
    decay_log = jnp.clip(-4.0 + 6.0 * jax.random.uniform(seeds[9], (NS, DI), jnp.float32) ** block_levels(seeds[9], (NS, DI), ((1, 8),), -0.2, 0.2), -4.0, 2.0)
    skip_gain = jnp.clip(1.0 + 0.15 * jax.random.normal(seeds[10], (DI,), jnp.float32), 0.25, 1.75)
    out_weight = gaussian_with(seeds[11], (DI, D), DI ** -0.5, 0.09375, ((0, 8),), (0, 1, 8, 2.0))
    norm_gain = jnp.clip(1.0 + 0.15 * jax.random.normal(seeds[12], (D,), jnp.float32), 0.25, 1.75)
    router = noise(seeds[13], (EXPERTS, D), D ** -0.5, 0.09375)
    expert_gate = noise(seeds[14], (FLIGHT, D, FF), D ** -0.5, 0.09375, ((0, 2), (2, 8)))
    expert_up = noise(seeds[15], (FLIGHT, D, FF), D ** -0.5, 0.09375, ((0, 2), (2, 8)))
    expert_down = gaussian_with(seeds[16], (FLIGHT, FF, D), FF ** -0.5, 0.078125, ((0, 2), (1, 8)), (1, 2, 8, 2.0))
    expert_ids = draw_expert_ids(jax.random.fold_in(jax.random.fold_in(seeds[18], part), 71), part)
    return {"stream": stream, "projected": projected, "conv_state": conv_state, "scan_state": scan_state, "conv_weight": conv_weight, "conv_bias": conv_bias, "state_proj": state_proj, "step_proj": step_proj, "step_bias": step_bias, "decay_log": decay_log, "skip_gain": skip_gain, "out_weight": out_weight, "norm_gain": norm_gain, "router": router, "expert_gate": expert_gate, "expert_up": expert_up, "expert_down": expert_down, "expert_ids": expert_ids}


def reference(stream, projected, conv_state, scan_state, conv_weight, conv_bias, state_proj, step_proj, step_bias, decay_log, skip_gain, out_weight, norm_gain, router, expert_gate, expert_up, expert_down, expert_ids):
    flat_rows = STEPS * ROWS
    inputs = projected[:, :, 0, :]
    gate_side = projected[:, :, 1, :]
    history = jnp.concatenate([conv_state.astype(jnp.float32), jnp.transpose(inputs, (1, 0, 2)).astype(jnp.float32)], axis=1)
    conv_list = []
    for step_no in range(STEPS):
        window = history[:, step_no:step_no + KC, :]
        conv_list.append(jax.nn.silu(lax.optimization_barrier(jnp.sum(window * conv_weight[None], axis=1)) + conv_bias).astype(jnp.bfloat16))
    convolved = jnp.stack(conv_list)
    projections = jnp.dot(convolved.reshape(flat_rows, DI), state_proj, preferred_element_type=jnp.float32).reshape(STEPS, ROWS, -1)
    low_rank = projections[..., :DTR].astype(jnp.bfloat16)
    input_gain = projections[..., DTR:DTR + NS]
    output_gain = projections[..., DTR + NS:]
    timestep = jax.nn.softplus(jnp.dot(low_rank.reshape(flat_rows, DTR), step_proj, preferred_element_type=jnp.float32).reshape(STEPS, ROWS, DI) + step_bias)
    decay_rates = jnp.exp(decay_log)
    carried = scan_state
    outputs = []
    for step_no in range(STEPS):
        current = convolved[step_no].astype(jnp.float32)
        delta_now = timestep[step_no]
        decay_now = jnp.exp(-delta_now[:, None, :] * decay_rates[None])
        carried = decay_now * carried + (delta_now * current)[:, None, :] * input_gain[step_no][:, :, None]
        readout = lax.optimization_barrier(jnp.sum(output_gain[step_no][:, :, None] * carried, axis=1)) + skip_gain * current
        outputs.append((readout * jax.nn.silu(gate_side[step_no].astype(jnp.float32))).astype(jnp.bfloat16))
    scanned = jnp.stack(outputs).reshape(flat_rows, DI)
    after_mamba = (stream.reshape(flat_rows, D).astype(jnp.float32) + jnp.dot(scanned, out_weight, preferred_element_type=jnp.float32)).astype(jnp.bfloat16)
    widened = after_mamba.astype(jnp.float32)
    normed = (widened * lax.rsqrt(lax.optimization_barrier(jnp.mean(widened * widened, axis=-1, keepdims=True)) + 1e-05) * norm_gain).astype(jnp.bfloat16)
    logits = jnp.dot(normed, router.T, preferred_element_type=jnp.float32)
    picked = expert_ids.reshape(flat_rows, TOPK)
    chosen = jnp.take_along_axis(logits, picked, axis=1)
    weights = jnp.exp(chosen)
    shares = weights / lax.optimization_barrier(jnp.sum(weights, axis=1, keepdims=True))
    combined = jnp.zeros((flat_rows, D), jnp.float32)
    slot_limit = STEPS * ROWS // 4
    for expert in range(expert_gate.shape[0]):
        weight_row = lax.optimization_barrier(jnp.sum(jnp.where(picked == expert, shares, 0.0), axis=1))
        routed = jnp.any(picked == expert, axis=1)
        index_list = jnp.nonzero(routed, size=slot_limit, fill_value=0)[0].astype(jnp.int32)
        live_count = jnp.sum(routed.astype(jnp.int32))
        valid_slot = (jnp.arange(slot_limit) < live_count).astype(jnp.float32)
        selected = normed[index_list]
        gate_part = jnp.dot(selected, expert_gate[expert], preferred_element_type=jnp.float32)
        up_part = jnp.dot(selected, expert_up[expert], preferred_element_type=jnp.float32)
        hidden = (jax.nn.silu(gate_part) * up_part).astype(jnp.bfloat16)
        result = jnp.dot(hidden, expert_down[expert], preferred_element_type=jnp.float32)
        contrib = (weight_row[index_list] * valid_slot)[:, None] * result
        combined = combined.at[index_list].add(contrib)
    mixed_out = (widened + combined).astype(jnp.bfloat16).reshape(STEPS, ROWS, D)
    return (mixed_out, carried)
```

```python
import functools

import jax
import jax.numpy as jnp
from jax import lax
from jax.experimental import pallas as pl
from jax.experimental.pallas import tpu as pltpu
from jax.sharding import PartitionSpec as P

CAP = 16
MESH = pl.DeviceIdType.MESH
F32 = jnp.float32
BF16 = jnp.bfloat16


def far_first(n):
    return sorted(range(1, n), key=lambda off: -min(off, n - off))


def sum_kernel(n, x_ref, o_ref, recv, own, send_a, recv_a, send_b, recv_b):
    me = lax.axis_index("mp")
    barrier = pltpu.get_barrier_semaphore()
    for off in range(1, n):
        pl.semaphore_signal(
            barrier, inc=1, device_id={"mp": lax.rem(me + off, n)}, device_id_type=MESH
        )
    pl.semaphore_wait(barrier, n - 1)
    order = far_first(n)
    first = {}
    for off in order:
        to = lax.rem(me + off, n)
        first[off] = pltpu.make_async_remote_copy(
            src_ref=x_ref.at[to],
            dst_ref=recv.at[off],
            send_sem=send_a.at[off],
            recv_sem=recv_a.at[off],
            device_id={"mp": to},
            device_id_type=MESH,
        )
        first[off].start()
    total = x_ref[me].astype(F32)
    for off in reversed(order):
        first[off].wait_recv()
        total = total + recv[off].astype(F32)
    own[...] = total.astype(own.dtype)
    second = {}
    for off in order:
        to = lax.rem(me + off, n)
        second[off] = pltpu.make_async_remote_copy(
            src_ref=own,
            dst_ref=o_ref.at[me],
            send_sem=send_b.at[off],
            recv_sem=recv_b.at[off],
            device_id={"mp": to},
            device_id_type=MESH,
        )
        second[off].start()
    o_ref[me] = own[...]
    for off in order:
        first[off].wait_send()
        second[off].wait()


def sum_over_mp(n, value):
    rows, cols = value.shape
    part = (rows // n, cols)
    dma = pltpu.SemaphoreType.DMA((n,))
    out = pl.pallas_call(
        functools.partial(sum_kernel, n),
        out_shape=jax.ShapeDtypeStruct((n,) + part, BF16),
        in_specs=[pl.BlockSpec(memory_space=pltpu.VMEM)],
        out_specs=pl.BlockSpec(memory_space=pltpu.VMEM),
        scratch_shapes=[
            pltpu.VMEM((n,) + part, BF16),
            pltpu.VMEM(part, BF16),
            dma,
            dma,
            dma,
            dma,
        ],
        compiler_params=pltpu.CompilerParams(collective_id=0, has_side_effects=True),
        name="sum_over_mp",
    )(value.astype(BF16).reshape((n,) + part))
    return out.reshape(rows, cols)


def tail_kernel(
    n,
    row_size,
    steps,
    tile,
    scanned,
    stream,
    gain,
    router,
    picked,
    picked_t,
    out_hbm,
    gate_hbm,
    up_hbm,
    down_hbm,
    o_ref,
    out_weight,
    gate,
    up,
    down,
    send1,
    recv1,
    stage,
    gathered,
    id_stage,
    ids,
    normed,
    hidden,
    send2,
    recv2,
    load_sem,
    s1,
    r1,
    s2,
    r2,
    si,
    ri,
    s3,
    r3,
):
    me = lax.axis_index("mp")
    row = lax.axis_index("row")
    flat, width = stream.shape
    full = normed.shape[1]
    slots = steps * CAP
    per_step = flat // steps
    peers = [(a, b) for b in [0] + far_first(n) for a in range(row_size) if a or b]

    def at(a, b):
        return {"row": lax.rem(row + a, row_size), "mp": lax.rem(me + b, n)}

    def cols(index):
        return pl.ds(pl.multiple_of(index * width, width), width)

    loads = [
        pltpu.make_async_copy(src, dst, load_sem.at[k])
        for k, (src, dst) in enumerate(
            [
                (out_hbm, out_weight),
                (gate_hbm.at[0], gate),
                (up_hbm.at[0], up),
                (down_hbm.at[0], down),
            ]
        )
    ]
    for load in loads:
        load.start()
    barrier = pltpu.get_barrier_semaphore()
    for a, b in peers:
        pl.semaphore_signal(barrier, inc=1, device_id=at(a, b), device_id_type=MESH)

    def iota(shape, dim):
        return lax.broadcasted_iota(jnp.int32, shape, dim)

    same_step = (iota((flat, flat), 0) // per_step) == (iota((flat, flat), 1) // per_step)
    lower = (same_step & (iota((flat, flat), 1) <= iota((flat, flat), 0))).astype(F32).astype(BF16)
    upper = (same_step & (iota((flat, flat), 0) <= iota((flat, flat), 1))).astype(F32).astype(BF16)
    choice = picked[...]
    choice_t = picked_t[...]
    top = choice.shape[1]
    select, spread = [], []
    for expert in range(row_size):
        hit_t = jnp.zeros((1, flat), F32)
        hit = jnp.zeros((flat, 1), F32)
        for k in range(top):
            hit_t = hit_t + (choice_t[k : k + 1, :] == expert).astype(F32)
            hit = hit + (choice[:, k : k + 1] == expert).astype(F32)
        count_t = jnp.dot(
            jnp.broadcast_to(hit_t, (slots, flat)).astype(BF16), upper, preferred_element_type=F32
        )
        slot = iota((slots, flat), 0)
        want = (slot % CAP + 1).astype(F32)
        ok = (slot // CAP == iota((slots, flat), 1) // per_step) & (count_t == want)
        select.append((ok.astype(F32) * hit_t).astype(BF16))
        count = jnp.dot(
            lower, jnp.broadcast_to(hit, (flat, slots)).astype(BF16), preferred_element_type=F32
        )
        slot = iota((flat, slots), 1)
        want = (slot % CAP + 1).astype(F32)
        ok = (slot // CAP == iota((flat, slots), 0) // per_step) & (count == want)
        spread.append((ok.astype(F32) * hit).astype(BF16))
    id_wide = jnp.concatenate(
        [jnp.broadcast_to(choice[:, k : k + 1], (flat, 128)) for k in range(top)], axis=1
    ).astype(F32).astype(BF16)
    for expert in range(row_size):
        id_stage[expert] = jnp.dot(
            select[expert], id_wide, preferred_element_type=F32
        ).astype(BF16)

    loads[0].wait()
    pl.semaphore_wait(barrier, len(peers))
    id_copies = []
    for a in range(1, row_size):
        copy = pltpu.make_async_remote_copy(
            src_ref=id_stage.at[lax.rem(row + a, row_size)],
            dst_ref=ids.at[row],
            send_sem=si.at[a],
            recv_sem=ri.at[a],
            device_id=at(a, 0),
            device_id_type=MESH,
        )
        copy.start()
        id_copies.append(copy)
    ids[row] = id_stage[row]
    first = {}
    for off in far_first(n):
        to = lax.rem(me + off, n)
        send1[off] = jnp.dot(
            scanned[...], out_weight[:, cols(to)], preferred_element_type=F32
        ).astype(BF16)
        first[off] = pltpu.make_async_remote_copy(
            src_ref=send1.at[off],
            dst_ref=recv1.at[off],
            send_sem=s1.at[off],
            recv_sem=r1.at[off],
            device_id=at(0, off),
            device_id_type=MESH,
        )
        first[off].start()
    total = stream[...].astype(F32) + jnp.dot(
        scanned[...], out_weight[:, cols(me)], preferred_element_type=F32
    )
    for off in reversed(far_first(n)):
        first[off].wait_recv()
        total = total + recv1[off].astype(F32)
    after = total.astype(BF16)

    for expert in range(row_size):
        stage[expert] = jnp.dot(select[expert], after, preferred_element_type=F32).astype(BF16)
    second = []
    for a, b in reversed(peers):
        copy = pltpu.make_async_remote_copy(
            src_ref=stage.at[lax.rem(row + a, row_size)],
            dst_ref=gathered.at[row, me],
            send_sem=s2.at[a, b],
            recv_sem=r2.at[a, b],
            device_id=at(a, b),
            device_id_type=MESH,
        )
        copy.start()
        second.append(copy)
    gathered[row, me] = stage[row]
    for copy in second:
        copy.wait_recv()
    for copy in id_copies:
        copy.wait_recv()
    for r in range(row_size):
        square = jnp.zeros((slots, 1), F32)
        for m in range(n):
            piece = gathered[r, m].astype(F32)
            square = square + jnp.sum(piece * piece, axis=1, keepdims=True)
        scale = lax.rsqrt(square / full + 1e-05)
        for m in range(n):
            piece = gathered[r, m].astype(F32)
            normed[r * slots : (r + 1) * slots, m * width : (m + 1) * width] = (
                piece * scale * gain[:, m * width : (m + 1) * width]
            ).astype(BF16)
    logits = lax.dot_general(
        normed[...], router[...], (((1,), (1,)), ((), ())), preferred_element_type=F32
    )
    slot_ids = jnp.concatenate([ids[r] for r in range(row_size)], axis=0).astype(F32)
    experts = logits.shape[1]
    column = iota(logits.shape, 1).astype(F32)
    mine = row.astype(F32)
    weight_sum = jnp.zeros((row_size * slots, 1), F32)
    weight_own = jnp.zeros((row_size * slots, 1), F32)
    for k in range(top):
        chosen_id = slot_ids[:, k * 128 : k * 128 + experts]
        chosen = jnp.sum(jnp.where(chosen_id == column, logits, 0.0), axis=1, keepdims=True)
        weight = jnp.exp(chosen)
        weight_sum = weight_sum + weight
        weight_own = weight_own + jnp.where(chosen_id[:, :1] == mine, weight, 0.0)
    share = weight_own / weight_sum

    loads[1].wait()
    loads[2].wait()

    def gate_up(i, carry):
        span = pl.ds(pl.multiple_of(i * tile, tile), tile)
        x = normed[...]
        g = jnp.dot(x, gate[:, span], preferred_element_type=F32)
        u = jnp.dot(x, up[:, span], preferred_element_type=F32)
        hidden[:, span] = (jax.nn.silu(g) * u).astype(BF16)
        return carry

    lax.fori_loop(0, gate.shape[1] // tile, gate_up, 0)
    loads[3].wait()
    third = []
    for b in far_first(n) + [0]:
        to = lax.rem(me + b, n)
        part = jnp.dot(hidden[...], down[:, cols(to)], preferred_element_type=F32) * share
        for r in range(row_size):
            send2[b, r] = part[r * slots : (r + 1) * slots].astype(BF16)
        for a in range(row_size):
            if a or b:
                copy = pltpu.make_async_remote_copy(
                    src_ref=send2.at[b, lax.rem(row + a, row_size)],
                    dst_ref=recv2.at[row, b],
                    send_sem=s3.at[a, b],
                    recv_sem=r3.at[a, b],
                    device_id=at(a, b),
                    device_id_type=MESH,
                )
                copy.start()
                third.append(copy)
    recv2[row, 0] = send2[0, row]
    for copy in third:
        copy.wait_recv()
    result = after.astype(F32)
    for expert in range(row_size):
        got = recv2[expert, 0].astype(F32)
        for b in range(1, n):
            got = got + recv2[expert, b].astype(F32)
        high = got.astype(BF16)
        low = (got - high.astype(F32)).astype(BF16)
        result = result + (
            jnp.dot(spread[expert], high, preferred_element_type=F32)
            + jnp.dot(spread[expert], low, preferred_element_type=F32)
        )
    o_ref[...] = result.astype(o_ref.dtype)
    for copy in id_copies + list(first.values()) + second + third:
        copy.wait_send()


def tail(n, row_size, steps, scanned, stream, gain, router, picked, out_w, gate_w, up_w, down_w):
    flat, width = stream.shape
    full = out_w.shape[1]
    slots = steps * CAP
    ff = gate_w.shape[2]
    tile = 256 if ff % 256 == 0 else 128
    dma = pltpu.SemaphoreType.DMA
    vmem = pl.BlockSpec(memory_space=pltpu.VMEM)
    hbm = pl.BlockSpec(memory_space=pl.ANY)
    return pl.pallas_call(
        functools.partial(tail_kernel, n, row_size, steps, tile),
        out_shape=jax.ShapeDtypeStruct((flat, width), BF16),
        in_specs=[vmem] * 6 + [hbm] * 4,
        out_specs=vmem,
        scratch_shapes=[
            pltpu.VMEM(out_w.shape, BF16),
            pltpu.VMEM(gate_w.shape[1:], BF16),
            pltpu.VMEM(up_w.shape[1:], BF16),
            pltpu.VMEM(down_w.shape[1:], BF16),
            pltpu.VMEM((n, flat, width), BF16),
            pltpu.VMEM((n, flat, width), BF16),
            pltpu.VMEM((row_size, slots, width), BF16),
            pltpu.VMEM((row_size, n, slots, width), BF16),
            pltpu.VMEM((row_size, slots, 128 * picked.shape[1]), BF16),
            pltpu.VMEM((row_size, slots, 128 * picked.shape[1]), BF16),
            pltpu.VMEM((row_size * slots, full), BF16),
            pltpu.VMEM((row_size * slots, ff), BF16),
            pltpu.VMEM((n, row_size, slots, width), BF16),
            pltpu.VMEM((row_size, n, slots, width), BF16),
            dma((4,)),
            dma((n,)),
            dma((n,)),
            dma((row_size, n)),
            dma((row_size, n)),
            dma((row_size,)),
            dma((row_size,)),
            dma((row_size, n)),
            dma((row_size, n)),
        ],
        compiler_params=pltpu.CompilerParams(
            collective_id=1, has_side_effects=True, vmem_limit_bytes=56 * 1024 * 1024
        ),
        name="tail",
    )(
        scanned,
        stream,
        gain.reshape(1, -1),
        router,
        picked,
        jnp.transpose(picked),
        out_w,
        gate_w,
        up_w,
        down_w,
    )


def on_device(
    stream,
    projected,
    conv_state,
    scan_state,
    conv_weight,
    conv_bias,
    state_proj,
    step_proj,
    step_bias,
    decay_log,
    skip_gain,
    out_weight,
    norm_gain,
    router,
    expert_gate,
    expert_up,
    expert_down,
    expert_ids,
):
    step_count, row_count, width_local = stream.shape
    inner_local = projected.shape[3]
    kernel_size = conv_weight.shape[0]
    rank_size = step_proj.shape[0]
    state_size = decay_log.shape[0]
    flat_rows = step_count * row_count
    inputs = projected[:, :, 0, :]
    gate_side = projected[:, :, 1, :]
    history = jnp.concatenate(
        [conv_state.astype(jnp.float32), jnp.transpose(inputs, (1, 0, 2)).astype(jnp.float32)],
        axis=1,
    )
    conv_list = []
    for step_no in range(step_count):
        window = history[:, step_no : step_no + kernel_size, :]
        conv_list.append(
            jax.nn.silu(jnp.sum(window * conv_weight[None], axis=1) + conv_bias).astype(
                jnp.bfloat16
            )
        )
    convolved = jnp.stack(conv_list)
    local_proj = jnp.dot(
        convolved.reshape(flat_rows, inner_local), state_proj, preferred_element_type=jnp.float32
    )
    projections = sum_over_mp(lax.axis_size("mp"), local_proj).reshape(
        step_count, row_count, -1
    )
    low_rank = projections[..., :rank_size].astype(jnp.bfloat16)
    input_gain = projections[..., rank_size : rank_size + state_size].astype(jnp.float32)
    output_gain = projections[..., rank_size + state_size :].astype(jnp.float32)
    timestep = jax.nn.softplus(
        jnp.dot(
            low_rank.reshape(flat_rows, rank_size), step_proj, preferred_element_type=jnp.float32
        ).reshape(step_count, row_count, inner_local)
        + step_bias
    )
    decay_rates = jnp.exp(decay_log)
    carried = scan_state
    outputs = []
    for step_no in range(step_count):
        current = convolved[step_no].astype(jnp.float32)
        delta_now = timestep[step_no]
        decay_now = jnp.exp(-delta_now[:, None, :] * decay_rates[None])
        carried = (
            decay_now * carried
            + (delta_now * current)[:, None, :] * input_gain[step_no][:, :, None]
        )
        readout = jnp.sum(output_gain[step_no][:, :, None] * carried, axis=1) + skip_gain * current
        outputs.append(
            (readout * jax.nn.silu(gate_side[step_no].astype(jnp.float32))).astype(jnp.bfloat16)
        )
    scanned = jnp.stack(outputs).reshape(flat_rows, inner_local)
    mixed_out = tail(
        lax.axis_size("mp"),
        lax.axis_size("row"),
        step_count,
        scanned,
        stream.reshape(flat_rows, width_local),
        norm_gain,
        router,
        expert_ids.reshape(flat_rows, -1),
        out_weight,
        expert_gate,
        expert_up,
        expert_down,
    ).reshape(step_count, row_count, width_local)
    return (mixed_out, carried)


def solution(mesh):
    return jax.shard_map(
        on_device,
        mesh=mesh,
        in_specs=(
            P(None, ("groups", "row"), "mp"),
            P(None, ("groups", "row"), None, "mp"),
            P(("groups", "row"), None, "mp"),
            P(("groups", "row"), None, "mp"),
            P(None, "mp"),
            P("mp"),
            P("mp", None),
            P(None, "mp"),
            P("mp"),
            P(None, "mp"),
            P("mp"),
            P("mp", None),
            P(),
            P(),
            P("row", None, "mp"),
            P("row", None, "mp"),
            P("row", "mp", None),
            P(None, ("groups", "row"), None),
        ),
        out_specs=(P(None, ("groups", "row"), "mp"), P(("groups", "row"), None, "mp")),
        check_vma=False,
    )
```

```python
import functools

import jax
import jax.numpy as jnp
from jax import lax
from jax.experimental import pallas as pl
from jax.experimental.pallas import tpu as pltpu
from jax.sharding import PartitionSpec as P

CAP = 16
MESH = pl.DeviceIdType.MESH
F32 = jnp.float32
BF16 = jnp.bfloat16


def far_first(n):
    return sorted(range(1, n), key=lambda off: -min(off, n - off))


def sum_kernel(n, x_ref, o_ref, recv, own, send_a, recv_a, send_b, recv_b):
    me = lax.axis_index("mp")
    barrier = pltpu.get_barrier_semaphore()
    for off in range(1, n):
        pl.semaphore_signal(
            barrier, inc=1, device_id={"mp": lax.rem(me + off, n)}, device_id_type=MESH
        )
    pl.semaphore_wait(barrier, n - 1)
    order = far_first(n)
    first = {}
    for off in order:
        to = lax.rem(me + off, n)
        first[off] = pltpu.make_async_remote_copy(
            src_ref=x_ref.at[to],
            dst_ref=recv.at[off],
            send_sem=send_a.at[off],
            recv_sem=recv_a.at[off],
            device_id={"mp": to},
            device_id_type=MESH,
        )
        first[off].start()
    total = x_ref[me].astype(F32)
    for off in reversed(order):
        first[off].wait_recv()
        total = total + recv[off].astype(F32)
    own[...] = total.astype(own.dtype)
    second = {}
    for off in order:
        to = lax.rem(me + off, n)
        second[off] = pltpu.make_async_remote_copy(
            src_ref=own,
            dst_ref=o_ref.at[me],
            send_sem=send_b.at[off],
            recv_sem=recv_b.at[off],
            device_id={"mp": to},
            device_id_type=MESH,
        )
        second[off].start()
    o_ref[me] = own[...]
    for off in order:
        first[off].wait_send()
        second[off].wait()


def sum_over_mp(n, value):
    rows, cols = value.shape
    part = (rows // n, cols)
    dma = pltpu.SemaphoreType.DMA((n,))
    out = pl.pallas_call(
        functools.partial(sum_kernel, n),
        out_shape=jax.ShapeDtypeStruct((n,) + part, BF16),
        in_specs=[pl.BlockSpec(memory_space=pltpu.VMEM)],
        out_specs=pl.BlockSpec(memory_space=pltpu.VMEM),
        scratch_shapes=[
            pltpu.VMEM((n,) + part, BF16),
            pltpu.VMEM(part, BF16),
            dma,
            dma,
            dma,
            dma,
        ],
        compiler_params=pltpu.CompilerParams(collective_id=0, has_side_effects=True),
        name="sum_over_mp",
    )(value.astype(BF16).reshape((n,) + part))
    return out.reshape(rows, cols)


def tail_kernel(
    n,
    row_size,
    steps,
    tile,
    scanned,
    stream,
    gain,
    router,
    picked,
    picked_t,
    out_hbm,
    gate_hbm,
    up_hbm,
    down_hbm,
    o_ref,
    out_weight,
    gate,
    up,
    down,
    send1,
    recv1,
    stage,
    gathered,
    id_stage,
    ids,
    normed,
    hidden,
    send2,
    recv2,
    load_sem,
    s1,
    r1,
    s2,
    r2,
    si,
    ri,
    s3,
    r3,
    cross1,
    met1,
    cross2,
    met2,
    sc1,
    rc1,
    sf,
    rf,
    sc2,
    rc2,
):
    me = lax.axis_index("mp")
    row = lax.axis_index("row")
    flat, width = stream.shape
    full = normed.shape[1]
    slots = steps * CAP
    per_step = flat // steps
    pairs = n // 2
    side = lax.rem(me, 2)
    place = me // 2
    order = far_first(pairs) + [0]
    peers = [(a, b) for b in reversed(order) for a in range(row_size) if a or b]

    def at(a, b):
        return {"row": lax.rem(row + a, row_size), "mp": lax.rem(place + b, pairs) * 2 + side}

    partner = {"row": row, "mp": place * 2 + 1 - side}

    def cols(index):
        return pl.ds(pl.multiple_of(index * width, width), width)

    loads = [
        pltpu.make_async_copy(src, dst, load_sem.at[k])
        for k, (src, dst) in enumerate(
            [
                (out_hbm, out_weight),
                (gate_hbm.at[0], gate),
                (up_hbm.at[0], up),
                (down_hbm.at[0], down),
            ]
        )
    ]
    for load in loads:
        load.start()
    barrier = pltpu.get_barrier_semaphore()
    for a, b in peers:
        pl.semaphore_signal(barrier, inc=1, device_id=at(a, b), device_id_type=MESH)
    pl.semaphore_signal(barrier, inc=1, device_id=partner, device_id_type=MESH)

    def iota(shape, dim):
        return lax.broadcasted_iota(jnp.int32, shape, dim)

    same_step = (iota((flat, flat), 0) // per_step) == (iota((flat, flat), 1) // per_step)
    lower = (same_step & (iota((flat, flat), 1) <= iota((flat, flat), 0))).astype(F32).astype(BF16)
    upper = (same_step & (iota((flat, flat), 0) <= iota((flat, flat), 1))).astype(F32).astype(BF16)
    choice = picked[...]
    choice_t = picked_t[...]
    top = choice.shape[1]
    select, spread = [], []
    for expert in range(row_size):
        hit_t = jnp.zeros((1, flat), F32)
        hit = jnp.zeros((flat, 1), F32)
        for k in range(top):
            hit_t = hit_t + (choice_t[k : k + 1, :] == expert).astype(F32)
            hit = hit + (choice[:, k : k + 1] == expert).astype(F32)
        count_t = jnp.dot(
            jnp.broadcast_to(hit_t, (slots, flat)).astype(BF16), upper, preferred_element_type=F32
        )
        slot = iota((slots, flat), 0)
        want = (slot % CAP + 1).astype(F32)
        ok = (slot // CAP == iota((slots, flat), 1) // per_step) & (count_t == want)
        select.append((ok.astype(F32) * hit_t).astype(BF16))
        count = jnp.dot(
            lower, jnp.broadcast_to(hit, (flat, slots)).astype(BF16), preferred_element_type=F32
        )
        slot = iota((flat, slots), 1)
        want = (slot % CAP + 1).astype(F32)
        ok = (slot // CAP == iota((flat, slots), 0) // per_step) & (count == want)
        spread.append((ok.astype(F32) * hit).astype(BF16))
    id_wide = jnp.concatenate(
        [jnp.broadcast_to(choice[:, k : k + 1], (flat, 128)) for k in range(top)], axis=1
    ).astype(F32).astype(BF16)
    for expert in range(row_size):
        id_stage[expert] = jnp.dot(
            select[expert], id_wide, preferred_element_type=F32
        ).astype(BF16)

    loads[0].wait()
    pl.semaphore_wait(barrier, len(peers) + 1)
    id_copies = []
    for a in range(1, row_size):
        copy = pltpu.make_async_remote_copy(
            src_ref=id_stage.at[lax.rem(row + a, row_size)],
            dst_ref=ids.at[row],
            send_sem=si.at[a],
            recv_sem=ri.at[a],
            device_id=at(a, 0),
            device_id_type=MESH,
        )
        copy.start()
        id_copies.append(copy)
    ids[row] = id_stage[row]
    across = {}
    for off in order:
        to = lax.rem(place + off, pairs) * 2 + 1 - side
        cross1[off] = jnp.dot(
            scanned[...], out_weight[:, cols(to)], preferred_element_type=F32
        ).astype(BF16)
        across[off] = pltpu.make_async_remote_copy(
            src_ref=cross1.at[off],
            dst_ref=met1.at[off],
            send_sem=sc1.at[off],
            recv_sem=rc1.at[off],
            device_id=partner,
            device_id_type=MESH,
        )
        across[off].start()
    first = {}
    for off in order:
        to = lax.rem(place + off, pairs) * 2 + side
        part = jnp.dot(scanned[...], out_weight[:, cols(to)], preferred_element_type=F32)
        across[off].wait_recv()
        part = part + met1[off].astype(F32)
        if off:
            send1[off] = part.astype(BF16)
            first[off] = pltpu.make_async_remote_copy(
                src_ref=send1.at[off],
                dst_ref=recv1.at[off],
                send_sem=s1.at[off],
                recv_sem=r1.at[off],
                device_id=at(0, off),
                device_id_type=MESH,
            )
            first[off].start()
        else:
            total = stream[...].astype(F32) + part
    for off in order[:-1]:
        first[off].wait_recv()
        total = total + recv1[off].astype(F32)
    after = total.astype(BF16)

    for expert in range(row_size):
        stage[expert] = jnp.dot(select[expert], after, preferred_element_type=F32).astype(BF16)
    second = {}
    for a, b in reversed(peers):
        second[a, b] = pltpu.make_async_remote_copy(
            src_ref=stage.at[lax.rem(row + a, row_size)],
            dst_ref=gathered.at[row, me],
            send_sem=s2.at[a, b],
            recv_sem=r2.at[a, b],
            device_id=at(a, b),
            device_id_type=MESH,
        )
        second[a, b].start()
    gathered[row, me] = stage[row]
    onward = []
    for a, b in [(0, 0)] + peers:
        r = lax.rem(row - a + row_size, row_size)
        m = lax.rem(place - b + pairs, pairs) * 2 + side
        if a or b:
            second[a, b].wait_recv()
            block = gathered.at[r, m]
        else:
            block = stage.at[row]
        copy = pltpu.make_async_remote_copy(
            src_ref=block,
            dst_ref=gathered.at[r, m],
            send_sem=sf.at[a, b],
            recv_sem=rf.at[a, b],
            device_id=partner,
            device_id_type=MESH,
        )
        copy.start()
        onward.append(copy)
    for copy in onward:
        copy.wait_recv()
    for copy in id_copies:
        copy.wait_recv()
    for r in range(row_size):
        square = jnp.zeros((slots, 1), F32)
        for m in range(n):
            piece = gathered[r, m].astype(F32)
            square = square + jnp.sum(piece * piece, axis=1, keepdims=True)
        scale = lax.rsqrt(square / full + 1e-05)
        for m in range(n):
            piece = gathered[r, m].astype(F32)
            normed[r * slots : (r + 1) * slots, m * width : (m + 1) * width] = (
                piece * scale * gain[:, m * width : (m + 1) * width]
            ).astype(BF16)
    logits = lax.dot_general(
        normed[...], router[...], (((1,), (1,)), ((), ())), preferred_element_type=F32
    )
    slot_ids = jnp.concatenate([ids[r] for r in range(row_size)], axis=0).astype(F32)
    experts = logits.shape[1]
    column = iota(logits.shape, 1).astype(F32)
    mine = row.astype(F32)
    weight_sum = jnp.zeros((row_size * slots, 1), F32)
    weight_own = jnp.zeros((row_size * slots, 1), F32)
    for k in range(top):
        chosen_id = slot_ids[:, k * 128 : k * 128 + experts]
        chosen = jnp.sum(jnp.where(chosen_id == column, logits, 0.0), axis=1, keepdims=True)
        weight = jnp.exp(chosen)
        weight_sum = weight_sum + weight
        weight_own = weight_own + jnp.where(chosen_id[:, :1] == mine, weight, 0.0)
    share = weight_own / weight_sum

    loads[1].wait()
    loads[2].wait()

    def gate_up(i, carry):
        span = pl.ds(pl.multiple_of(i * tile, tile), tile)
        x = normed[...]
        g = jnp.dot(x, gate[:, span], preferred_element_type=F32)
        u = jnp.dot(x, up[:, span], preferred_element_type=F32)
        hidden[:, span] = (jax.nn.silu(g) * u).astype(BF16)
        return carry

    lax.fori_loop(0, gate.shape[1] // tile, gate_up, 0)
    loads[3].wait()
    back = {}
    for b in order:
        to = lax.rem(place + b, pairs) * 2 + 1 - side
        cross2[b] = (
            jnp.dot(hidden[...], down[:, cols(to)], preferred_element_type=F32) * share
        ).astype(BF16)
        back[b] = pltpu.make_async_remote_copy(
            src_ref=cross2.at[b],
            dst_ref=met2.at[b],
            send_sem=sc2.at[b],
            recv_sem=rc2.at[b],
            device_id=partner,
            device_id_type=MESH,
        )
        back[b].start()
    third = []
    for b in order:
        to = lax.rem(place + b, pairs) * 2 + side
        part = jnp.dot(hidden[...], down[:, cols(to)], preferred_element_type=F32) * share
        back[b].wait_recv()
        part = part + met2[b].astype(F32)
        for r in range(row_size):
            send2[b, r] = part[r * slots : (r + 1) * slots].astype(BF16)
        for a in range(row_size):
            if a or b:
                copy = pltpu.make_async_remote_copy(
                    src_ref=send2.at[b, lax.rem(row + a, row_size)],
                    dst_ref=recv2.at[row, b],
                    send_sem=s3.at[a, b],
                    recv_sem=r3.at[a, b],
                    device_id=at(a, b),
                    device_id_type=MESH,
                )
                copy.start()
                third.append(copy)
    recv2[row, 0] = send2[0, row]
    for copy in third:
        copy.wait_recv()
    result = after.astype(F32)
    for expert in range(row_size):
        got = recv2[expert, 0].astype(F32)
        for b in range(1, pairs):
            got = got + recv2[expert, b].astype(F32)
        high = got.astype(BF16)
        low = (got - high.astype(F32)).astype(BF16)
        result = result + (
            jnp.dot(spread[expert], high, preferred_element_type=F32)
            + jnp.dot(spread[expert], low, preferred_element_type=F32)
        )
    o_ref[...] = result.astype(o_ref.dtype)
    sent = [across, first, second, back]
    for copy in id_copies + [c for group in sent for c in group.values()] + onward + third:
        copy.wait_send()


def tail(n, row_size, steps, scanned, stream, gain, router, picked, out_w, gate_w, up_w, down_w):
    flat, width = stream.shape
    full = out_w.shape[1]
    slots = steps * CAP
    ff = gate_w.shape[2]
    tile = 256 if ff % 256 == 0 else 128
    pairs = n // 2
    dma = pltpu.SemaphoreType.DMA
    vmem = pl.BlockSpec(memory_space=pltpu.VMEM)
    hbm = pl.BlockSpec(memory_space=pl.ANY)
    return pl.pallas_call(
        functools.partial(tail_kernel, n, row_size, steps, tile),
        out_shape=jax.ShapeDtypeStruct((flat, width), BF16),
        in_specs=[vmem] * 6 + [hbm] * 4,
        out_specs=vmem,
        scratch_shapes=[
            pltpu.VMEM(out_w.shape, BF16),
            pltpu.VMEM(gate_w.shape[1:], BF16),
            pltpu.VMEM(up_w.shape[1:], BF16),
            pltpu.VMEM(down_w.shape[1:], BF16),
            pltpu.VMEM((pairs, flat, width), BF16),
            pltpu.VMEM((pairs, flat, width), BF16),
            pltpu.VMEM((row_size, slots, width), BF16),
            pltpu.VMEM((row_size, n, slots, width), BF16),
            pltpu.VMEM((row_size, slots, 128 * picked.shape[1]), BF16),
            pltpu.VMEM((row_size, slots, 128 * picked.shape[1]), BF16),
            pltpu.VMEM((row_size * slots, full), BF16),
            pltpu.VMEM((row_size * slots, ff), BF16),
            pltpu.VMEM((pairs, row_size, slots, width), BF16),
            pltpu.VMEM((row_size, pairs, slots, width), BF16),
            dma((4,)),
            dma((pairs,)),
            dma((pairs,)),
            dma((row_size, pairs)),
            dma((row_size, pairs)),
            dma((row_size,)),
            dma((row_size,)),
            dma((row_size, pairs)),
            dma((row_size, pairs)),
            pltpu.VMEM((pairs, flat, width), BF16),
            pltpu.VMEM((pairs, flat, width), BF16),
            pltpu.VMEM((pairs, row_size * slots, width), BF16),
            pltpu.VMEM((pairs, row_size * slots, width), BF16),
            dma((pairs,)),
            dma((pairs,)),
            dma((row_size, pairs)),
            dma((row_size, pairs)),
            dma((pairs,)),
            dma((pairs,)),
        ],
        compiler_params=pltpu.CompilerParams(
            collective_id=1, has_side_effects=True, vmem_limit_bytes=56 * 1024 * 1024
        ),
        name="tail",
    )(
        scanned,
        stream,
        gain.reshape(1, -1),
        router,
        picked,
        jnp.transpose(picked),
        out_w,
        gate_w,
        up_w,
        down_w,
    )


def on_device(
    stream,
    projected,
    conv_state,
    scan_state,
    conv_weight,
    conv_bias,
    state_proj,
    step_proj,
    step_bias,
    decay_log,
    skip_gain,
    out_weight,
    norm_gain,
    router,
    expert_gate,
    expert_up,
    expert_down,
    expert_ids,
):
    step_count, row_count, width_local = stream.shape
    inner_local = projected.shape[3]
    kernel_size = conv_weight.shape[0]
    rank_size = step_proj.shape[0]
    state_size = decay_log.shape[0]
    flat_rows = step_count * row_count
    inputs = projected[:, :, 0, :]
    gate_side = projected[:, :, 1, :]
    history = jnp.concatenate(
        [conv_state.astype(jnp.float32), jnp.transpose(inputs, (1, 0, 2)).astype(jnp.float32)],
        axis=1,
    )
    conv_list = []
    for step_no in range(step_count):
        window = history[:, step_no : step_no + kernel_size, :]
        conv_list.append(
            jax.nn.silu(jnp.sum(window * conv_weight[None], axis=1) + conv_bias).astype(
                jnp.bfloat16
            )
        )
    convolved = jnp.stack(conv_list)
    local_proj = jnp.dot(
        convolved.reshape(flat_rows, inner_local), state_proj, preferred_element_type=jnp.float32
    )
    projections = sum_over_mp(lax.axis_size("mp"), local_proj).reshape(
        step_count, row_count, -1
    )
    low_rank = projections[..., :rank_size].astype(jnp.bfloat16)
    input_gain = projections[..., rank_size : rank_size + state_size].astype(jnp.float32)
    output_gain = projections[..., rank_size + state_size :].astype(jnp.float32)
    timestep = jax.nn.softplus(
        jnp.dot(
            low_rank.reshape(flat_rows, rank_size), step_proj, preferred_element_type=jnp.float32
        ).reshape(step_count, row_count, inner_local)
        + step_bias
    )
    decay_rates = jnp.exp(decay_log)
    carried = scan_state
    outputs = []
    for step_no in range(step_count):
        current = convolved[step_no].astype(jnp.float32)
        delta_now = timestep[step_no]
        decay_now = jnp.exp(-delta_now[:, None, :] * decay_rates[None])
        carried = (
            decay_now * carried
            + (delta_now * current)[:, None, :] * input_gain[step_no][:, :, None]
        )
        readout = jnp.sum(output_gain[step_no][:, :, None] * carried, axis=1) + skip_gain * current
        outputs.append(
            (readout * jax.nn.silu(gate_side[step_no].astype(jnp.float32))).astype(jnp.bfloat16)
        )
    scanned = jnp.stack(outputs).reshape(flat_rows, inner_local)
    mixed_out = tail(
        lax.axis_size("mp"),
        lax.axis_size("row"),
        step_count,
        scanned,
        stream.reshape(flat_rows, width_local),
        norm_gain,
        router,
        expert_ids.reshape(flat_rows, -1),
        out_weight,
        expert_gate,
        expert_up,
        expert_down,
    ).reshape(step_count, row_count, width_local)
    return (mixed_out, carried)


def solution(mesh):
    return jax.shard_map(
        on_device,
        mesh=mesh,
        in_specs=(
            P(None, ("groups", "row"), "mp"),
            P(None, ("groups", "row"), None, "mp"),
            P(("groups", "row"), None, "mp"),
            P(("groups", "row"), None, "mp"),
            P(None, "mp"),
            P("mp"),
            P("mp", None),
            P(None, "mp"),
            P("mp"),
            P(None, "mp"),
            P("mp"),
            P("mp", None),
            P(),
            P(),
            P("row", None, "mp"),
            P("row", None, "mp"),
            P("row", "mp", None),
            P(None, ("groups", "row"), None),
        ),
        out_specs=(P(None, ("groups", "row"), "mp"), P(("groups", "row"), None, "mp")),
        check_vma=False,
    )
```

```python
import functools

import jax
import jax.numpy as jnp
from jax import lax
from jax.experimental import pallas as pl
from jax.experimental.pallas import tpu as pltpu
from jax.sharding import PartitionSpec as P

CAP = 16
LANES = 128
MESH = pl.DeviceIdType.MESH
F32 = jnp.float32
BF16 = jnp.bfloat16


def far_first(n):
    return sorted(range(1, n), key=lambda off: -min(off, n - off))


def kernel(
    n,
    row_size,
    tile,
    xz,
    conv_state,
    conv_weight,
    conv_bias,
    state_proj,
    step_proj,
    step_bias,
    decay_log,
    skip_gain,
    stream,
    gain,
    router,
    picked,
    state_hbm,
    out_hbm,
    gate_hbm,
    up_hbm,
    down_hbm,
    o_ref,
    new_state,
    state,
    convolved,
    delta,
    moved,
    readout,
    gain_in,
    gain_out,
    rates,
    part_proj,
    recv_proj,
    own_proj,
    full_proj,
    out_weight,
    gate,
    up,
    down,
    send1,
    recv1,
    stage,
    gathered,
    id_stage,
    ids,
    normed,
    hidden,
    send2,
    recv2,
    cross1,
    met1,
    cross2,
    met2,
    load_sem,
    sa,
    ra,
    sb,
    rb,
    s1,
    r1,
    s2,
    r2,
    si,
    ri,
    s3,
    r3,
    sc1,
    rc1,
    sf,
    rf,
    sc2,
    rc2,
):
    me = lax.axis_index("mp")
    row = lax.axis_index("row")
    steps, rows, width = stream.shape
    flat = steps * rows
    inner = xz.shape[3]
    taps = conv_weight.shape[0]
    rank = step_proj.shape[0]
    entries = decay_log.shape[0]
    full = normed.shape[1]
    slots = steps * CAP
    pairs = n // 2
    side = lax.rem(me, 2)
    place = me // 2
    order = far_first(pairs) + [0]
    peers = [(a, b) for b in reversed(order) for a in range(row_size) if a or b]

    def at(a, b):
        return {"row": lax.rem(row + a, row_size), "mp": lax.rem(place + b, pairs) * 2 + side}

    partner = {"row": row, "mp": place * 2 + 1 - side}

    def along(off):
        return {"row": row, "mp": lax.rem(me + off, n)}

    def cols(index):
        return pl.ds(pl.multiple_of(index * width, width), width)

    loads = [
        pltpu.make_async_copy(src, dst, load_sem.at[k])
        for k, (src, dst) in enumerate(
            [
                (out_hbm, out_weight),
                (gate_hbm.at[0], gate),
                (up_hbm.at[0], up),
                (down_hbm.at[0], down),
                (state_hbm, state),
            ]
        )
    ]
    barrier = pltpu.get_barrier_semaphore()
    for off in far_first(n):
        pl.semaphore_signal(barrier, inc=1, device_id=along(off), device_id_type=MESH)
    others = [(a, b) for a, b in peers if a]
    for a, b in others:
        pl.semaphore_signal(barrier, inc=1, device_id=at(a, b), device_id_type=MESH)
    for k in (4, 0, 1, 2, 3):
        loads[k].start()

    window = [conv_state[k].astype(F32) for k in range(taps - 1)]
    window = window + [xz[0, s].astype(F32) for s in range(steps)]
    local = []
    for s in range(steps):
        total = conv_bias[...]
        for k in range(taps):
            total = total + window[s + k] * conv_weight[k : k + 1, :]
        convolved[s] = jax.nn.silu(total).astype(BF16)
        local.append(
            lax.dot_general(
                convolved[s],
                state_proj[...],
                (((1,), (1,)), ((), ())),
                preferred_element_type=F32,
            )
        )
    local = jnp.concatenate(local, axis=0)
    piece = flat // n
    for k in range(n):
        part_proj[k] = local[k * piece : (k + 1) * piece].astype(BF16)
    pl.semaphore_wait(barrier, n - 1 + len(others))
    spread_out = {}
    for off in far_first(n):
        spread_out[off] = pltpu.make_async_remote_copy(
            src_ref=part_proj.at[lax.rem(me + off, n)],
            dst_ref=recv_proj.at[off],
            send_sem=sa.at[off],
            recv_sem=ra.at[off],
            device_id=along(off),
            device_id_type=MESH,
        )
        spread_out[off].start()

    def iota(shape, dim):
        return lax.broadcasted_iota(jnp.int32, shape, dim)

    rates[...] = -jnp.exp(decay_log[...])
    same_step = (iota((flat, flat), 0) // rows) == (iota((flat, flat), 1) // rows)
    upper = (same_step & (iota((flat, flat), 0) <= iota((flat, flat), 1))).astype(F32).astype(BF16)
    top = picked.shape[1]
    choice = [
        jnp.concatenate([picked[s, k : k + 1, :] for s in range(steps)], axis=1)
        for k in range(top)
    ]
    select = []
    for expert in range(row_size):
        hit = jnp.zeros((1, flat), F32)
        for k in range(top):
            hit = hit + (choice[k] == expert).astype(F32)
        count = jnp.dot(
            jnp.broadcast_to(hit, (slots, flat)).astype(BF16), upper, preferred_element_type=F32
        )
        slot = iota((slots, flat), 0)
        want = (slot % CAP + 1).astype(F32)
        ok = (slot // CAP == iota((slots, flat), 1) // rows) & (count == want)
        chosen = ok.astype(F32) * hit
        select.append(chosen.astype(BF16))
        for k in range(top):
            slot_id = jnp.sum(chosen * choice[k].astype(F32), axis=1, keepdims=True)
            id_stage[expert, :, k * LANES : (k + 1) * LANES] = jnp.broadcast_to(
                slot_id, (slots, LANES)
            ).astype(BF16)
    id_copies = []
    for a in range(1, row_size):
        copy = pltpu.make_async_remote_copy(
            src_ref=id_stage.at[lax.rem(row + a, row_size)],
            dst_ref=ids.at[row],
            send_sem=si.at[a],
            recv_sem=ri.at[a],
            device_id=at(a, 0),
            device_id_type=MESH,
        )
        copy.start()
        id_copies.append(copy)
    ids[row] = id_stage[row]

    total = part_proj[me].astype(F32)
    for off in reversed(far_first(n)):
        spread_out[off].wait_recv()
        total = total + recv_proj[off].astype(F32)
    own_proj[...] = total.astype(BF16)
    collect = {}
    for off in far_first(n):
        collect[off] = pltpu.make_async_remote_copy(
            src_ref=own_proj,
            dst_ref=full_proj.at[me],
            send_sem=sb.at[off],
            recv_sem=rb.at[off],
            device_id=along(off),
            device_id_type=MESH,
        )
        collect[off].start()
    full_proj[me] = own_proj[...]
    for off in reversed(far_first(n)):
        collect[off].wait_recv()
    summed = jnp.concatenate([full_proj[k].astype(F32) for k in range(n)], axis=0)
    raw = (
        jnp.dot(summed[:, :rank].astype(BF16), step_proj[...], preferred_element_type=F32)
        + step_bias[...]
    )
    soft = jnp.maximum(raw, 0.0) + jnp.log1p(jnp.exp(-jnp.abs(raw)))
    for s in range(steps):
        step_now = soft[s * rows : (s + 1) * rows]
        delta[s] = step_now
        moved[s] = step_now * convolved[s].astype(F32)
        for k in range(entries):
            column = summed[s * rows : (s + 1) * rows, rank + k : rank + k + 1]
            gain_in[s, :, k, :] = jnp.broadcast_to(column, (rows, LANES))
            column = summed[
                s * rows : (s + 1) * rows, rank + entries + k : rank + entries + k + 1
            ]
            gain_out[s, :, k, :] = jnp.broadcast_to(column, (rows, LANES))

    loads[4].wait()
    across = {}
    scanned = []
    for s in range(steps):

        def scan_rows(block, carry, s=s):
            start = pl.multiple_of(block * 8, 8)
            for c in range(0, inner, LANES):
                lane = slice(c, c + LANES)
                step_now = delta[s, pl.ds(start, 8), lane]
                moved_now = moved[s, pl.ds(start, 8), lane]
                lines = []
                for j in range(8):
                    held = (
                        jnp.exp(step_now[j : j + 1] * rates[:, lane]) * state[start + j, :, lane]
                        + moved_now[j : j + 1] * gain_in[s, start + j]
                    )
                    state[start + j, :, lane] = held
                    lines.append(
                        jnp.sum(gain_out[s, start + j] * held, axis=0, keepdims=True)
                    )
                readout[pl.ds(start, 8), lane] = jnp.concatenate(lines, axis=0)
            return carry

        lax.fori_loop(0, rows // 8, scan_rows, 0)
        result = readout[...] + skip_gain[...] * convolved[s].astype(F32)
        scanned.append((result * jax.nn.silu(xz[1, s].astype(F32))).astype(BF16))
        if s == 0:
            loads[0].wait()
        for off in order:
            to = lax.rem(place + off, pairs) * 2 + 1 - side
            cross1[s, off] = jnp.dot(
                scanned[s], out_weight[:, cols(to)], preferred_element_type=F32
            ).astype(BF16)
            across[s, off] = pltpu.make_async_remote_copy(
                src_ref=cross1.at[s, off],
                dst_ref=met1.at[s, off],
                send_sem=sc1.at[s, off],
                recv_sem=rc1.at[s, off],
                device_id=partner,
                device_id_type=MESH,
            )
            across[s, off].start()
    write_state = pltpu.make_async_copy(state, new_state, load_sem.at[5])
    write_state.start()
    first = {}
    totals = []
    for s in range(steps):
        for off in order:
            to = lax.rem(place + off, pairs) * 2 + side
            part = jnp.dot(scanned[s], out_weight[:, cols(to)], preferred_element_type=F32)
            across[s, off].wait_recv()
            part = part + met1[s, off].astype(F32)
            if off:
                send1[s, off] = part.astype(BF16)
                first[s, off] = pltpu.make_async_remote_copy(
                    src_ref=send1.at[s, off],
                    dst_ref=recv1.at[s, off],
                    send_sem=s1.at[s, off],
                    recv_sem=r1.at[s, off],
                    device_id=at(0, off),
                    device_id_type=MESH,
                )
                first[s, off].start()
            else:
                totals.append(stream[s].astype(F32) + part)
    for s in range(steps):
        for off in reversed(order[:-1]):
            first[s, off].wait_recv()
            totals[s] = totals[s] + recv1[s, off].astype(F32)
    after = jnp.concatenate(totals, axis=0).astype(BF16)

    for expert in range(row_size):
        stage[expert] = jnp.dot(select[expert], after, preferred_element_type=F32).astype(BF16)
    second = {}
    for a, b in reversed(peers):
        second[a, b] = pltpu.make_async_remote_copy(
            src_ref=stage.at[lax.rem(row + a, row_size)],
            dst_ref=gathered.at[row, me],
            send_sem=s2.at[a, b],
            recv_sem=r2.at[a, b],
            device_id=at(a, b),
            device_id_type=MESH,
        )
        second[a, b].start()
    gathered[row, me] = stage[row]
    onward = []
    for a, b in [(0, 0)] + peers:
        r = lax.rem(row - a + row_size, row_size)
        m = lax.rem(place - b + pairs, pairs) * 2 + side
        if a or b:
            second[a, b].wait_recv()
            block = gathered.at[r, m]
        else:
            block = stage.at[row]
        copy = pltpu.make_async_remote_copy(
            src_ref=block,
            dst_ref=gathered.at[r, m],
            send_sem=sf.at[a, b],
            recv_sem=rf.at[a, b],
            device_id=partner,
            device_id_type=MESH,
        )
        copy.start()
        onward.append(copy)
    for copy in onward:
        copy.wait_recv()
    for copy in id_copies:
        copy.wait_recv()
    for r in range(row_size):
        square = jnp.zeros((slots, 1), F32)
        for m in range(n):
            piece = gathered[r, m].astype(F32)
            square = square + jnp.sum(piece * piece, axis=1, keepdims=True)
        scale = lax.rsqrt(square / full + 1e-05)
        for m in range(n):
            piece = gathered[r, m].astype(F32)
            normed[r * slots : (r + 1) * slots, m * width : (m + 1) * width] = (
                piece * scale * gain[:, m * width : (m + 1) * width]
            ).astype(BF16)
    logits = lax.dot_general(
        normed[...], router[...], (((1,), (1,)), ((), ())), preferred_element_type=F32
    )
    slot_ids = jnp.concatenate([ids[r] for r in range(row_size)], axis=0).astype(F32)
    experts = logits.shape[1]
    column = iota(logits.shape, 1).astype(F32)
    mine = row.astype(F32)
    weight_sum = jnp.zeros((row_size * slots, 1), F32)
    weight_own = jnp.zeros((row_size * slots, 1), F32)
    for k in range(top):
        chosen_id = slot_ids[:, k * LANES : k * LANES + experts]
        chosen = jnp.sum(jnp.where(chosen_id == column, logits, 0.0), axis=1, keepdims=True)
        weight = jnp.exp(chosen)
        weight_sum = weight_sum + weight
        weight_own = weight_own + jnp.where(chosen_id[:, :1] == mine, weight, 0.0)
    share = weight_own / weight_sum

    loads[1].wait()
    loads[2].wait()

    def gate_up(i, carry):
        span = pl.ds(pl.multiple_of(i * tile, tile), tile)
        x = normed[...]
        g = jnp.dot(x, gate[:, span], preferred_element_type=F32)
        u = jnp.dot(x, up[:, span], preferred_element_type=F32)
        hidden[:, span] = (jax.nn.silu(g) * u).astype(BF16)
        return carry

    lax.fori_loop(0, gate.shape[1] // tile, gate_up, 0)
    loads[3].wait()
    back = {}
    for b in order:
        to = lax.rem(place + b, pairs) * 2 + 1 - side
        cross2[b] = (
            jnp.dot(hidden[...], down[:, cols(to)], preferred_element_type=F32) * share
        ).astype(BF16)
        back[b] = pltpu.make_async_remote_copy(
            src_ref=cross2.at[b],
            dst_ref=met2.at[b],
            send_sem=sc2.at[b],
            recv_sem=rc2.at[b],
            device_id=partner,
            device_id_type=MESH,
        )
        back[b].start()
    third = []
    for b in order:
        to = lax.rem(place + b, pairs) * 2 + side
        part = jnp.dot(hidden[...], down[:, cols(to)], preferred_element_type=F32) * share
        back[b].wait_recv()
        part = part + met2[b].astype(F32)
        for r in range(row_size):
            send2[b, r] = part[r * slots : (r + 1) * slots].astype(BF16)
        for a in range(row_size):
            if a or b:
                copy = pltpu.make_async_remote_copy(
                    src_ref=send2.at[b, lax.rem(row + a, row_size)],
                    dst_ref=recv2.at[row, b],
                    send_sem=s3.at[a, b],
                    recv_sem=r3.at[a, b],
                    device_id=at(a, b),
                    device_id_type=MESH,
                )
                copy.start()
                third.append(copy)
    recv2[row, 0] = send2[0, row]
    for copy in third:
        copy.wait_recv()
    combined = jnp.zeros((flat, width), F32)
    for expert in range(row_size):
        got = recv2[expert, 0].astype(F32)
        for b in range(1, pairs):
            got = got + recv2[expert, b].astype(F32)
        high = got.astype(BF16)
        low = (got - high.astype(F32)).astype(BF16)
        for piece_now in (high, low):
            combined = combined + lax.dot_general(
                select[expert],
                piece_now,
                (((0,), (0,)), ((), ())),
                preferred_element_type=F32,
            )
    mixed = after.astype(F32) + combined
    for s in range(steps):
        o_ref[s] = mixed[s * rows : (s + 1) * rows].astype(o_ref.dtype)
    sent = [spread_out, collect, across, first, second, back]
    for copy in id_copies + [c for group in sent for c in group.values()] + onward + third:
        copy.wait_send()
    write_state.wait()


def on_device(
    stream,
    projected,
    conv_state,
    scan_state,
    conv_weight,
    conv_bias,
    state_proj,
    step_proj,
    step_bias,
    decay_log,
    skip_gain,
    out_weight,
    norm_gain,
    router,
    expert_gate,
    expert_up,
    expert_down,
    expert_ids,
):
    n = lax.axis_size("mp")
    row_size = lax.axis_size("row")
    steps, rows, width = stream.shape
    inner = projected.shape[3]
    entries = decay_log.shape[0]
    columns = state_proj.shape[1]
    full = out_weight.shape[1]
    ff = expert_gate.shape[2]
    top = expert_ids.shape[2]
    flat = steps * rows
    slots = steps * CAP
    pairs = n // 2
    piece = flat // n
    tile = 256 if ff % 256 == 0 else 128
    dma = pltpu.SemaphoreType.DMA
    vmem = pl.BlockSpec(memory_space=pltpu.VMEM)
    hbm = pl.BlockSpec(memory_space=pl.ANY)

    def half(*shape):
        return pltpu.VMEM(shape, BF16)

    def wide(*shape):
        return pltpu.VMEM(shape, F32)

    return pl.pallas_call(
        functools.partial(kernel, n, row_size, tile),
        out_shape=(
            jax.ShapeDtypeStruct(stream.shape, stream.dtype),
            jax.ShapeDtypeStruct(scan_state.shape, scan_state.dtype),
        ),
        in_specs=[vmem] * 13 + [hbm] * 5,
        out_specs=(vmem, hbm),
        scratch_shapes=[
            wide(rows, entries, inner),
            half(steps, rows, inner),
            wide(steps, rows, inner),
            wide(steps, rows, inner),
            wide(rows, inner),
            wide(steps, rows, entries, LANES),
            wide(steps, rows, entries, LANES),
            wide(entries, inner),
            half(n, piece, columns),
            half(n, piece, columns),
            half(piece, columns),
            half(n, piece, columns),
            half(*out_weight.shape),
            half(*expert_gate.shape[1:]),
            half(*expert_up.shape[1:]),
            half(*expert_down.shape[1:]),
            half(steps, pairs, rows, width),
            half(steps, pairs, rows, width),
            half(row_size, slots, width),
            half(row_size, n, slots, width),
            half(row_size, slots, LANES * top),
            half(row_size, slots, LANES * top),
            half(row_size * slots, full),
            half(row_size * slots, ff),
            half(pairs, row_size, slots, width),
            half(row_size, pairs, slots, width),
            half(steps, pairs, rows, width),
            half(steps, pairs, rows, width),
            half(pairs, row_size * slots, width),
            half(pairs, row_size * slots, width),
            dma((6,)),
            dma((n,)),
            dma((n,)),
            dma((n,)),
            dma((n,)),
            dma((steps, pairs)),
            dma((steps, pairs)),
            dma((row_size, pairs)),
            dma((row_size, pairs)),
            dma((row_size,)),
            dma((row_size,)),
            dma((row_size, pairs)),
            dma((row_size, pairs)),
            dma((steps, pairs)),
            dma((steps, pairs)),
            dma((row_size, pairs)),
            dma((row_size, pairs)),
            dma((pairs,)),
            dma((pairs,)),
        ],
        compiler_params=pltpu.CompilerParams(
            collective_id=0, has_side_effects=True, vmem_limit_bytes=62 * 1024 * 1024
        ),
        name="decode",
    )(
        jnp.transpose(projected, (2, 0, 1, 3)),
        jnp.transpose(conv_state, (1, 0, 2)),
        conv_weight,
        conv_bias.reshape(1, -1),
        jnp.transpose(state_proj),
        step_proj,
        step_bias.reshape(1, -1),
        decay_log,
        skip_gain.reshape(1, -1),
        stream,
        norm_gain.reshape(1, -1),
        router,
        jnp.transpose(expert_ids, (0, 2, 1)),
        scan_state,
        out_weight,
        expert_gate,
        expert_up,
        expert_down,
    )


def solution(mesh):
    return jax.shard_map(
        on_device,
        mesh=mesh,
        in_specs=(
            P(None, ("groups", "row"), "mp"),
            P(None, ("groups", "row"), None, "mp"),
            P(("groups", "row"), None, "mp"),
            P(("groups", "row"), None, "mp"),
            P(None, "mp"),
            P("mp"),
            P("mp", None),
            P(None, "mp"),
            P("mp"),
            P(None, "mp"),
            P("mp"),
            P("mp", None),
            P(),
            P(),
            P("row", None, "mp"),
            P("row", None, "mp"),
            P("row", "mp", None),
            P(None, ("groups", "row"), None),
        ),
        out_specs=(P(None, ("groups", "row"), "mp"), P(("groups", "row"), None, "mp")),
        check_vma=False,
    )
```

```python
import functools

import jax
import jax.numpy as jnp
from jax import lax
from jax.experimental import pallas as pl
from jax.experimental.pallas import tpu as pltpu
from jax.sharding import PartitionSpec as P

CAP = 16
LANES = 128
MESH = pl.DeviceIdType.MESH
F32 = jnp.float32
BF16 = jnp.bfloat16


def far_first(n):
    return sorted(range(1, n), key=lambda off: -min(off, n - off))


def kernel(
    n,
    row_size,
    tile,
    xz,
    conv_state,
    conv_weight,
    conv_bias,
    state_proj,
    step_proj,
    step_bias,
    decay_log,
    skip_gain,
    stream,
    gain,
    router,
    picked,
    state_hbm,
    out_hbm,
    gate_hbm,
    up_hbm,
    down_hbm,
    o_ref,
    state,
    convolved,
    delta,
    moved,
    readout,
    gain_in,
    gain_out,
    rates,
    part_proj,
    recv_proj,
    own_proj,
    full_proj,
    out_weight,
    gate,
    up,
    down,
    send1,
    recv1,
    stage,
    gathered,
    id_stage,
    ids,
    normed,
    hidden,
    send2,
    recv2,
    cross1,
    met1,
    cross2,
    met2,
    load_sem,
    sa,
    ra,
    sb,
    rb,
    s1,
    r1,
    s2,
    r2,
    si,
    ri,
    s3,
    r3,
    sc1,
    rc1,
    sf,
    rf,
    sc2,
    rc2,
):
    me = lax.axis_index("mp")
    row = lax.axis_index("row")
    steps, rows, width = stream.shape
    flat = steps * rows
    inner = xz.shape[3]
    taps = conv_weight.shape[0]
    rank = step_proj.shape[0]
    entries = decay_log.shape[0]
    full = normed.shape[1]
    slots = steps * CAP
    pairs = n // 2
    side = lax.rem(me, 2)
    place = me // 2
    order = far_first(pairs) + [0]
    peers = [(a, b) for b in reversed(order) for a in range(row_size) if a or b]

    def at(a, b):
        return {"row": lax.rem(row + a, row_size), "mp": lax.rem(place + b, pairs) * 2 + side}

    partner = {"row": row, "mp": place * 2 + 1 - side}

    def along(off):
        return {"row": row, "mp": lax.rem(me + off, n)}

    def cols(index):
        return pl.ds(pl.multiple_of(index * width, width), width)

    loads = [
        pltpu.make_async_copy(src, dst, load_sem.at[k])
        for k, (src, dst) in enumerate(
            [
                (out_hbm, out_weight),
                (gate_hbm.at[0], gate),
                (up_hbm.at[0], up),
                (down_hbm.at[0], down),
                (state_hbm, state),
            ]
        )
    ]
    barrier = pltpu.get_barrier_semaphore()
    for off in far_first(n):
        pl.semaphore_signal(barrier, inc=1, device_id=along(off), device_id_type=MESH)
    others = [(a, b) for a, b in peers if a]
    for a, b in others:
        pl.semaphore_signal(barrier, inc=1, device_id=at(a, b), device_id_type=MESH)
    for k in (4, 0, 1, 2, 3):
        loads[k].start()

    window = [conv_state[k].astype(F32) for k in range(taps - 1)]
    window = window + [xz[0, s].astype(F32) for s in range(steps)]
    local = []
    for s in range(steps):
        total = conv_bias[...]
        for k in range(taps):
            total = total + window[s + k] * conv_weight[k : k + 1, :]
        convolved[s] = jax.nn.silu(total).astype(BF16)
        local.append(
            lax.dot_general(
                convolved[s],
                state_proj[...],
                (((1,), (1,)), ((), ())),
                preferred_element_type=F32,
            )
        )
    local = jnp.concatenate(local, axis=0)
    piece = flat // n
    for k in range(n):
        part_proj[k] = local[k * piece : (k + 1) * piece].astype(BF16)
    pl.semaphore_wait(barrier, n - 1 + len(others))
    spread_out = {}
    for off in far_first(n):
        spread_out[off] = pltpu.make_async_remote_copy(
            src_ref=part_proj.at[lax.rem(me + off, n)],
            dst_ref=recv_proj.at[off],
            send_sem=sa.at[off],
            recv_sem=ra.at[off],
            device_id=along(off),
            device_id_type=MESH,
        )
        spread_out[off].start()

    def iota(shape, dim):
        return lax.broadcasted_iota(jnp.int32, shape, dim)

    rates[...] = -jnp.exp(decay_log[...])
    same_step = (iota((flat, flat), 0) // rows) == (iota((flat, flat), 1) // rows)
    upper = (same_step & (iota((flat, flat), 0) <= iota((flat, flat), 1))).astype(F32).astype(BF16)
    top = picked.shape[1]
    choice = [
        jnp.concatenate([picked[s, k : k + 1, :] for s in range(steps)], axis=1)
        for k in range(top)
    ]
    select = []
    for expert in range(row_size):
        hit = jnp.zeros((1, flat), F32)
        for k in range(top):
            hit = hit + (choice[k] == expert).astype(F32)
        count = jnp.dot(
            jnp.broadcast_to(hit, (slots, flat)).astype(BF16), upper, preferred_element_type=F32
        )
        slot = iota((slots, flat), 0)
        want = (slot % CAP + 1).astype(F32)
        ok = (slot // CAP == iota((slots, flat), 1) // rows) & (count == want)
        chosen = ok.astype(F32) * hit
        select.append(chosen.astype(BF16))
        for k in range(top):
            slot_id = jnp.sum(chosen * choice[k].astype(F32), axis=1, keepdims=True)
            id_stage[expert, :, k * LANES : (k + 1) * LANES] = jnp.broadcast_to(
                slot_id, (slots, LANES)
            ).astype(BF16)
    id_copies = []
    for a in range(1, row_size):
        copy = pltpu.make_async_remote_copy(
            src_ref=id_stage.at[lax.rem(row + a, row_size)],
            dst_ref=ids.at[row],
            send_sem=si.at[a],
            recv_sem=ri.at[a],
            device_id=at(a, 0),
            device_id_type=MESH,
        )
        copy.start()
        id_copies.append(copy)
    ids[row] = id_stage[row]

    total = part_proj[me].astype(F32)
    for off in reversed(far_first(n)):
        spread_out[off].wait_recv()
        total = total + recv_proj[off].astype(F32)
    own_proj[...] = total.astype(BF16)
    collect = {}
    for off in far_first(n):
        collect[off] = pltpu.make_async_remote_copy(
            src_ref=own_proj,
            dst_ref=full_proj.at[me],
            send_sem=sb.at[off],
            recv_sem=rb.at[off],
            device_id=along(off),
            device_id_type=MESH,
        )
        collect[off].start()
    full_proj[me] = own_proj[...]
    for off in reversed(far_first(n)):
        collect[off].wait_recv()
    summed = jnp.concatenate([full_proj[k].astype(F32) for k in range(n)], axis=0)
    raw = (
        jnp.dot(summed[:, :rank].astype(BF16), step_proj[...], preferred_element_type=F32)
        + step_bias[...]
    )
    soft = jnp.maximum(raw, 0.0) + jnp.log1p(jnp.exp(-jnp.abs(raw)))
    for s in range(steps):
        step_now = soft[s * rows : (s + 1) * rows]
        delta[s] = step_now
        moved[s] = step_now * convolved[s].astype(F32)
        for k in range(entries):
            column = summed[s * rows : (s + 1) * rows, rank + k : rank + k + 1]
            gain_in[s, :, k, :] = jnp.broadcast_to(column, (rows, LANES))
            column = summed[
                s * rows : (s + 1) * rows, rank + entries + k : rank + entries + k + 1
            ]
            gain_out[s, :, k, :] = jnp.broadcast_to(column, (rows, LANES))

    loads[4].wait()
    across = {}
    scanned = []
    for s in range(steps):

        def scan_rows(block, carry, s=s):
            start = pl.multiple_of(block * 8, 8)
            for c in range(0, inner, LANES):
                lane = slice(c, c + LANES)
                step_now = delta[s, pl.ds(start, 8), lane]
                moved_now = moved[s, pl.ds(start, 8), lane]
                lines = []
                for j in range(8):
                    held = (
                        jnp.exp(step_now[j : j + 1] * rates[:, lane]) * state[start + j, :, lane]
                        + moved_now[j : j + 1] * gain_in[s, start + j]
                    )
                    state[start + j, :, lane] = held
                    lines.append(
                        jnp.sum(gain_out[s, start + j] * held, axis=0, keepdims=True)
                    )
                readout[pl.ds(start, 8), lane] = jnp.concatenate(lines, axis=0)
            return carry

        lax.fori_loop(0, rows // 8, scan_rows, 0)
        result = readout[...] + skip_gain[...] * convolved[s].astype(F32)
        scanned.append((result * jax.nn.silu(xz[1, s].astype(F32))).astype(BF16))
        if s == 0:
            loads[0].wait()
        for off in order:
            to = lax.rem(place + off, pairs) * 2 + 1 - side
            cross1[s, off] = jnp.dot(
                scanned[s], out_weight[:, cols(to)], preferred_element_type=F32
            ).astype(BF16)
            across[s, off] = pltpu.make_async_remote_copy(
                src_ref=cross1.at[s, off],
                dst_ref=met1.at[s, off],
                send_sem=sc1.at[s, off],
                recv_sem=rc1.at[s, off],
                device_id=partner,
                device_id_type=MESH,
            )
            across[s, off].start()
    first = {}
    totals = []
    for s in range(steps):
        for off in order:
            to = lax.rem(place + off, pairs) * 2 + side
            part = jnp.dot(scanned[s], out_weight[:, cols(to)], preferred_element_type=F32)
            across[s, off].wait_recv()
            part = part + met1[s, off].astype(F32)
            if off:
                send1[s, off] = part.astype(BF16)
                first[s, off] = pltpu.make_async_remote_copy(
                    src_ref=send1.at[s, off],
                    dst_ref=recv1.at[s, off],
                    send_sem=s1.at[s, off],
                    recv_sem=r1.at[s, off],
                    device_id=at(0, off),
                    device_id_type=MESH,
                )
                first[s, off].start()
            else:
                totals.append(stream[s].astype(F32) + part)
    for s in range(steps):
        for off in reversed(order[:-1]):
            first[s, off].wait_recv()
            totals[s] = totals[s] + recv1[s, off].astype(F32)
    after = jnp.concatenate(totals, axis=0).astype(BF16)

    for expert in range(row_size):
        stage[expert] = jnp.dot(select[expert], after, preferred_element_type=F32).astype(BF16)
    second = {}
    for a, b in reversed(peers):
        second[a, b] = pltpu.make_async_remote_copy(
            src_ref=stage.at[lax.rem(row + a, row_size)],
            dst_ref=gathered.at[row, me],
            send_sem=s2.at[a, b],
            recv_sem=r2.at[a, b],
            device_id=at(a, b),
            device_id_type=MESH,
        )
        second[a, b].start()
    gathered[row, me] = stage[row]
    onward = []
    for a, b in [(0, 0)] + peers:
        r = lax.rem(row - a + row_size, row_size)
        m = lax.rem(place - b + pairs, pairs) * 2 + side
        if a or b:
            second[a, b].wait_recv()
            block = gathered.at[r, m]
        else:
            block = stage.at[row]
        copy = pltpu.make_async_remote_copy(
            src_ref=block,
            dst_ref=gathered.at[r, m],
            send_sem=sf.at[a, b],
            recv_sem=rf.at[a, b],
            device_id=partner,
            device_id_type=MESH,
        )
        copy.start()
        onward.append(copy)
    for copy in onward:
        copy.wait_recv()
    for copy in id_copies:
        copy.wait_recv()
    for r in range(row_size):
        square = jnp.zeros((slots, 1), F32)
        for m in range(n):
            piece = gathered[r, m].astype(F32)
            square = square + jnp.sum(piece * piece, axis=1, keepdims=True)
        scale = lax.rsqrt(square / full + 1e-05)
        for m in range(n):
            piece = gathered[r, m].astype(F32)
            normed[r * slots : (r + 1) * slots, m * width : (m + 1) * width] = (
                piece * scale * gain[:, m * width : (m + 1) * width]
            ).astype(BF16)
    logits = lax.dot_general(
        normed[...], router[...], (((1,), (1,)), ((), ())), preferred_element_type=F32
    )
    slot_ids = jnp.concatenate([ids[r] for r in range(row_size)], axis=0).astype(F32)
    experts = logits.shape[1]
    column = iota(logits.shape, 1).astype(F32)
    mine = row.astype(F32)
    weight_sum = jnp.zeros((row_size * slots, 1), F32)
    weight_own = jnp.zeros((row_size * slots, 1), F32)
    for k in range(top):
        chosen_id = slot_ids[:, k * LANES : k * LANES + experts]
        chosen = jnp.sum(jnp.where(chosen_id == column, logits, 0.0), axis=1, keepdims=True)
        weight = jnp.exp(chosen)
        weight_sum = weight_sum + weight
        weight_own = weight_own + jnp.where(chosen_id[:, :1] == mine, weight, 0.0)
    share = weight_own / weight_sum

    loads[1].wait()
    loads[2].wait()

    def gate_up(i, carry):
        span = pl.ds(pl.multiple_of(i * tile, tile), tile)
        x = normed[...]
        g = jnp.dot(x, gate[:, span], preferred_element_type=F32)
        u = jnp.dot(x, up[:, span], preferred_element_type=F32)
        hidden[:, span] = (jax.nn.silu(g) * u).astype(BF16)
        return carry

    lax.fori_loop(0, gate.shape[1] // tile, gate_up, 0)
    loads[3].wait()
    back = {}
    for b in order:
        to = lax.rem(place + b, pairs) * 2 + 1 - side
        cross2[b] = (
            jnp.dot(hidden[...], down[:, cols(to)], preferred_element_type=F32) * share
        ).astype(BF16)
        back[b] = pltpu.make_async_remote_copy(
            src_ref=cross2.at[b],
            dst_ref=met2.at[b],
            send_sem=sc2.at[b],
            recv_sem=rc2.at[b],
            device_id=partner,
            device_id_type=MESH,
        )
        back[b].start()
    third = []
    for b in order:
        to = lax.rem(place + b, pairs) * 2 + side
        part = jnp.dot(hidden[...], down[:, cols(to)], preferred_element_type=F32) * share
        back[b].wait_recv()
        part = part + met2[b].astype(F32)
        for r in range(row_size):
            send2[b, r] = part[r * slots : (r + 1) * slots].astype(BF16)
        for a in range(row_size):
            if a or b:
                copy = pltpu.make_async_remote_copy(
                    src_ref=send2.at[b, lax.rem(row + a, row_size)],
                    dst_ref=recv2.at[row, b],
                    send_sem=s3.at[a, b],
                    recv_sem=r3.at[a, b],
                    device_id=at(a, b),
                    device_id_type=MESH,
                )
                copy.start()
                third.append(copy)
    recv2[row, 0] = send2[0, row]
    for copy in third:
        copy.wait_recv()
    combined = jnp.zeros((flat, width), F32)
    for expert in range(row_size):
        got = recv2[expert, 0].astype(F32)
        for b in range(1, pairs):
            got = got + recv2[expert, b].astype(F32)
        high = got.astype(BF16)
        low = (got - high.astype(F32)).astype(BF16)
        for piece_now in (high, low):
            combined = combined + lax.dot_general(
                select[expert],
                piece_now,
                (((0,), (0,)), ((), ())),
                preferred_element_type=F32,
            )
    mixed = after.astype(F32) + combined
    for s in range(steps):
        o_ref[s] = mixed[s * rows : (s + 1) * rows].astype(o_ref.dtype)
    sent = [spread_out, collect, across, first, second, back]
    for copy in id_copies + [c for group in sent for c in group.values()] + onward + third:
        copy.wait_send()


def on_device(
    stream,
    projected,
    conv_state,
    scan_state,
    conv_weight,
    conv_bias,
    state_proj,
    step_proj,
    step_bias,
    decay_log,
    skip_gain,
    out_weight,
    norm_gain,
    router,
    expert_gate,
    expert_up,
    expert_down,
    expert_ids,
):
    n = lax.axis_size("mp")
    row_size = lax.axis_size("row")
    steps, rows, width = stream.shape
    inner = projected.shape[3]
    entries = decay_log.shape[0]
    columns = state_proj.shape[1]
    full = out_weight.shape[1]
    ff = expert_gate.shape[2]
    top = expert_ids.shape[2]
    flat = steps * rows
    slots = steps * CAP
    pairs = n // 2
    piece = flat // n
    tile = 256 if ff % 256 == 0 else 128
    dma = pltpu.SemaphoreType.DMA
    vmem = pl.BlockSpec(memory_space=pltpu.VMEM)
    hbm = pl.BlockSpec(memory_space=pl.ANY)

    def half(*shape):
        return pltpu.VMEM(shape, BF16)

    def wide(*shape):
        return pltpu.VMEM(shape, F32)

    return pl.pallas_call(
        functools.partial(kernel, n, row_size, tile),
        out_shape=(
            half(*stream.shape),
            wide(*scan_state.shape),
        ),
        in_specs=[vmem] * 13 + [hbm] * 5,
        out_specs=(vmem, vmem),
        scratch_shapes=[
            half(steps, rows, inner),
            wide(steps, rows, inner),
            wide(steps, rows, inner),
            wide(rows, inner),
            wide(steps, rows, entries, LANES),
            wide(steps, rows, entries, LANES),
            wide(entries, inner),
            half(n, piece, columns),
            half(n, piece, columns),
            half(piece, columns),
            half(n, piece, columns),
            half(*out_weight.shape),
            half(*expert_gate.shape[1:]),
            half(*expert_up.shape[1:]),
            half(*expert_down.shape[1:]),
            half(steps, pairs, rows, width),
            half(steps, pairs, rows, width),
            half(row_size, slots, width),
            half(row_size, n, slots, width),
            half(row_size, slots, LANES * top),
            half(row_size, slots, LANES * top),
            half(row_size * slots, full),
            half(row_size * slots, ff),
            half(pairs, row_size, slots, width),
            half(row_size, pairs, slots, width),
            half(steps, pairs, rows, width),
            half(steps, pairs, rows, width),
            half(pairs, row_size * slots, width),
            half(pairs, row_size * slots, width),
            dma((5,)),
            dma((n,)),
            dma((n,)),
            dma((n,)),
            dma((n,)),
            dma((steps, pairs)),
            dma((steps, pairs)),
            dma((row_size, pairs)),
            dma((row_size, pairs)),
            dma((row_size,)),
            dma((row_size,)),
            dma((row_size, pairs)),
            dma((row_size, pairs)),
            dma((steps, pairs)),
            dma((steps, pairs)),
            dma((row_size, pairs)),
            dma((row_size, pairs)),
            dma((pairs,)),
            dma((pairs,)),
        ],
        compiler_params=pltpu.CompilerParams(
            collective_id=0, has_side_effects=True, vmem_limit_bytes=57 * 1024 * 1024
        ),
        name="decode",
    )(
        jnp.transpose(projected, (2, 0, 1, 3)),
        jnp.transpose(conv_state, (1, 0, 2)),
        conv_weight,
        conv_bias.reshape(1, -1),
        jnp.transpose(state_proj),
        step_proj,
        step_bias.reshape(1, -1),
        decay_log,
        skip_gain.reshape(1, -1),
        stream,
        norm_gain.reshape(1, -1),
        router,
        jnp.transpose(expert_ids, (0, 2, 1)),
        scan_state,
        out_weight,
        expert_gate,
        expert_up,
        expert_down,
    )


def solution(mesh):
    return jax.shard_map(
        on_device,
        mesh=mesh,
        in_specs=(
            P(None, ("groups", "row"), "mp"),
            P(None, ("groups", "row"), None, "mp"),
            P(("groups", "row"), None, "mp"),
            P(("groups", "row"), None, "mp"),
            P(None, "mp"),
            P("mp"),
            P("mp", None),
            P(None, "mp"),
            P("mp"),
            P(None, "mp"),
            P("mp"),
            P("mp", None),
            P(),
            P(),
            P("row", None, "mp"),
            P("row", None, "mp"),
            P("row", "mp", None),
            P(None, ("groups", "row"), None),
        ),
        out_specs=(P(None, ("groups", "row"), "mp"), P(("groups", "row"), None, "mp")),
        check_vma=False,
    )
```
